256 devices in a mesh: req: 64 (over z, x, core), tp: 4 (over y).
Axes of the slice: x: 4, y: 4, z: 8, core: 2. Of those that a mesh axis runs over, the one named last changes fastest.
Arguments:
- tokens: bfloat16 [16384, 1280], P('req'), as said below
- attention_gain: bfloat16 [1280], replicated, may hold values from 0.099609375 to 1.8984375
- feedforward_gain: bfloat16 [1280], replicated, may hold values from 0.099609375 to 1.8984375
- query_weight: bfloat16 [1280, 1280], P(None, 'tp'), may hold values from -0.15625 to 0.15625
- key_weight: bfloat16 [1280, 1280], P(None, 'tp'), may hold values from -0.625 to 0.625
- value_weight: bfloat16 [1280, 1280], P(None, 'tp'), may hold values from -0.3125 to 0.3125
- out_weight: bfloat16 [1280, 1280], P('tp'), may hold values from -0.3125 to 0.3125
- up_weight: bfloat16 [1280, 1280], P(None, 'tp'), may hold values from -0.15625 to 0.15625
- down_weight: bfloat16 [1280, 1280], P('tp'), may hold values from -0.15625 to 0.15625
- cache_keys: bfloat16 [64, 16, 192, 1280], P('req', None, None, 'tp'), as said below
- cache_values: bfloat16 [64, 16, 192, 1280], P('req', None, None, 'tp'), may hold values from -12 to 12
- request_prefix: int32 [128], replicated, may hold values from 0 to 15
- suffix_length: int32 [128], replicated, may hold values from 1 to 128, as said below
Outputs:
- layer_out: bfloat16 [16384, 1280], P('req', 'tp')
The draws below stay inside these ranges and needn't reach their ends.
Inputs may be any that keep to these rules, and one draw needn't show every extreme that they name: `suffix_length`: requests d * 2 to d * 2 + 1 are those of index d of req; their lengths sum to at most 192, on some index exactly 192; some request has exactly 128. `cache_keys`: keys of the cached prefix patches. `tokens`: patch embeddings.
All inputs are finite; a program needn't handle non-finite values.
Results may differ from the reference program's by a relative error of at most 0.0055.
The reference program's roundings to bfloat16 on the way (of `normed`, `attention`, `middle`, `normed_middle` and `hidden`) count: a program that leaves them out, or rounds other values in their place, can miss the bound.
Values may be sent and summed in bfloat16 or wider, within the bound.
No kernel may reach another device: no remote copies, remote signals or barrier semaphores. Data moves between devices by JAX's collectives and lax.ppermute only.
A program may use at most 128 MiB of HBM per device.

```python
import math
import jax
import jax.numpy as jnp
import numpy as np
from jax import lax

D = 1280
HEADS = 16
HDIM = 80
FF = 1280
PREFIXES = 16
SLOT = 128
R_DEV = 2
PG = 192
REQUESTS = 128
ROWS = 16384
LIVE = 192


def draw_tokens(key, part):
    first, second = jax.random.split(key, 2)
    row_scale = jnp.exp(jax.random.uniform(first, (ROWS, 1), jnp.float32, math.log(0.3), math.log(3.0)))
    column_scale = jnp.exp(math.log(0.3) + math.log(10.0) * jnp.arange(D, dtype=jnp.float32) / D)
    base = jax.random.normal(second, (ROWS, D), jnp.float32)
    return (base * row_scale * column_scale[None, :]).astype(jnp.bfloat16)


def draw_cache_keys(key, part):
    shape = (REQUESTS // R_DEV, PREFIXES, PG, D)
    first = jax.random.fold_in(key, 0)
    return (4.0 * jax.random.normal(first, shape, jnp.float32)).astype(jnp.bfloat16)


def draw_suffix_length(key, part):
    owner_count = REQUESTS // R_DEV
    first, second, third = jax.random.split(key, 3)
    factor_one = jax.random.randint(first, (owner_count, R_DEV), 0, SLOT)
    factor_two = jax.random.randint(second, (owner_count, R_DEV), 0, SLOT)
    raw_length = 1 + factor_one * factor_two // SLOT
    ranks = jnp.arange(R_DEV, dtype=jnp.int32)

    def cap_step(used, column):
        raw_column, rank = column
        room = LIVE - used - (R_DEV - 1 - rank)
        taken = jnp.minimum(raw_column, room)
        return (used + taken, taken)
    _, taken_all = lax.scan(cap_step, jnp.zeros((owner_count,), jnp.int32), (raw_length.T, ranks))
    lengths = taken_all.T
    chosen = jax.random.randint(third, (), 0, owner_count)
    remainder = LIVE - SLOT
    even_part = remainder // (R_DEV - 1)
    extra = jnp.where(ranks == R_DEV - 1, remainder - even_part * (R_DEV - 1), 0)
    full_row = jnp.where(ranks == 0, SLOT, even_part + extra)
    selected = (jnp.arange(owner_count) == chosen)[:, None]
    lengths = jnp.where(selected, full_row[None, :], lengths)
    return lengths.reshape(-1).astype(jnp.int32)


def plant(values, rng, least, high):
    extent = values.shape
    place = [jax.random.randint(jax.random.fold_in(rng, axis), (), 0, extent[axis]) for axis in range(len(extent))]
    values = values.at[tuple(place)].set(least)
    longest = extent.index(max(extent))
    place[longest] = (place[longest] + 1) % extent[longest]
    return values.at[tuple(place)].set(high)


def level_of(rng, shape, cuts, least, high):
    loudness, own = 1.0, jax.random.fold_in(rng, 6)
    for dim, blocks in cuts:
        heights = jnp.exp(jax.random.uniform(jax.random.fold_in(own, dim), (blocks,), jnp.float32, least / len(cuts), high / len(cuts)))
        loudness = loudness * jnp.repeat(heights, shape[dim] // blocks).reshape([-1 if axis == dim else 1 for axis in range(len(shape))])
    return loudness


def rank_table(count, lean):
    loads = [(1 << 20) // math.isqrt(standing ** lean) + 1 for standing in range(1, count + 1)]
    deviation = 1 + sum(loads) // (1 << 30)
    return np.cumsum(np.array([max(1, weight // deviation) for weight in loads]))


def ranked(key, shape, amount, skew):
    table = rank_table(amount, skew)
    pick = jax.random.randint(jax.random.fold_in(key, 1), shape, 0, int(table[amount - 1]))
    rank = jnp.searchsorted(jnp.asarray(table, jnp.int32), pick, side="right")
    return jax.random.permutation(jax.random.fold_in(key, 2), amount)[rank].astype(jnp.int32)


def bell_draw(stream_key, extent, scale, bound, shards=(), held_as=jnp.bfloat16):
    array = jax.random.normal(stream_key, extent, jnp.float32) * scale
    if len(shards) > 0:
        array = level_of(stream_key, extent, shards, -0.22, 0.18) * array
    return jnp.clip(array, min=-bound, max=bound).astype(held_as)


def setup_inputs(seed: int = 0) -> dict:
    key_list = jax.random.split(jax.random.key(seed), 14)
    tokens = draw_tokens(jax.random.fold_in(key_list[13], 71), 0)
    attention_gain = jnp.clip(1.0 + 0.18 * jax.random.normal(key_list[1], (D,), jnp.float32), 0.099609375, 1.8984375).astype(jnp.bfloat16)
    feedforward_gain = jnp.clip(1.0 + 0.18 * jax.random.normal(key_list[2], (D,), jnp.float32), 0.099609375, 1.8984375).astype(jnp.bfloat16)
    query_weight = bell_draw(key_list[3], (D, D), D ** -0.5, 0.15625, ((1, 4),))
    key_weight = bell_draw(key_list[4], (D, D), (D // 16) ** -0.5, 0.625, ((1, 4),))
    value_weight = bell_draw(key_list[5], (D, D), (D // 4) ** -0.5, 0.3125, ((1, 4),))
    out_weight = bell_draw(key_list[6], (D, D), (D // 4) ** -0.5, 0.3125, ((0, 4),))
    up_weight = bell_draw(key_list[7], (D, FF), D ** -0.5, 0.15625, ((1, 4),))
    down_weight = bell_draw(key_list[8], (FF, D), FF ** -0.5, 0.15625, ((0, 4),))
    cache_keys = draw_cache_keys(jax.random.fold_in(key_list[13], 71), 0)
    cache_values = bell_draw(key_list[10], (REQUESTS // R_DEV, PREFIXES, PG, D), 2.0, 12.0, ((0, 64), (3, 4)))
    request_prefix = plant(ranked(key_list[11], (REQUESTS,), PREFIXES, 2), jax.random.fold_in(key_list[11], 3), 0, PREFIXES - 1).astype(jnp.int32)
    suffix_length = draw_suffix_length(jax.random.fold_in(key_list[13], 71), 0)
    return dict(tokens=tokens, attention_gain=attention_gain, feedforward_gain=feedforward_gain, query_weight=query_weight, key_weight=key_weight, value_weight=value_weight, out_weight=out_weight, up_weight=up_weight, down_weight=down_weight, cache_keys=cache_keys, cache_values=cache_values, request_prefix=request_prefix, suffix_length=suffix_length)


EPSILON = 1e-06
NEGATIVE = -1e+30

def normalize(values, gain):
    floats = values.astype(jnp.float32)
    mean_square = lax.optimization_barrier(jnp.mean(floats * floats, axis=-1, keepdims=True))
    return (floats * lax.rsqrt(mean_square + EPSILON) * gain.astype(jnp.float32)).astype(jnp.bfloat16)

def rounded(values):
    return lax.optimization_barrier(values.astype(jnp.bfloat16)).astype(jnp.float32)

def reference(tokens, attention_gain, feedforward_gain, query_weight, key_weight, value_weight, out_weight, up_weight, down_weight, cache_keys, cache_values, request_prefix, suffix_length):
    score_scale = 1.0 / math.sqrt(HDIM)
    normed = normalize(tokens, attention_gain)
    queries = jnp.dot(normed, query_weight, preferred_element_type=jnp.float32).astype(jnp.bfloat16)
    keys_own = jnp.dot(normed, key_weight, preferred_element_type=jnp.float32).astype(jnp.bfloat16)
    values_own = jnp.dot(normed, value_weight, preferred_element_type=jnp.float32).astype(jnp.bfloat16)
    query_slots = queries.astype(jnp.float32).reshape(REQUESTS, SLOT, HEADS, HDIM)
    key_slots = keys_own.astype(jnp.float32).reshape(REQUESTS, SLOT, HEADS, HDIM)
    value_slots = values_own.astype(jnp.float32).reshape(REQUESTS, SLOT, HEADS, HDIM)
    own_scores = jnp.einsum('rqhe,rkhe->rhqk', query_slots, key_slots) * score_scale
    causal = jnp.arange(SLOT)[:, None] >= jnp.arange(SLOT)[None, :]
    own_scores = jnp.where(causal[None, None], own_scores, NEGATIVE)
    own_top = lax.optimization_barrier(jnp.max(own_scores, axis=-1))
    own_weights = jnp.exp(own_scores - own_top[..., None])
    own_total = lax.optimization_barrier(jnp.sum(own_weights, axis=-1))
    own_numer = jnp.einsum('rhqk,rkhe->rhqe', rounded(own_weights), value_slots)

    def owner_step(carry, owner):
        row_peak, denominator, numerator = carry
        keys_owner = lax.dynamic_index_in_dim(cache_keys, owner, 0, keepdims=False)[request_prefix]
        values_owner = lax.dynamic_index_in_dim(cache_values, owner, 0, keepdims=False)[request_prefix]
        keys_owner = keys_owner.astype(jnp.float32).reshape(REQUESTS, PG, HEADS, HDIM)
        values_owner = values_owner.astype(jnp.float32).reshape(REQUESTS, PG, HEADS, HDIM)
        scores = jnp.einsum('rqhe,rkhe->rhqk', query_slots, keys_owner) * score_scale
        top_value = rounded(lax.optimization_barrier(jnp.max(scores, axis=-1)))
        weights = jnp.exp(scores - top_value[..., None])
        total_mass = lax.optimization_barrier(jnp.sum(weights, axis=-1))
        numer_owner = jnp.einsum('rhqk,rkhe->rhqe', rounded(weights), values_owner)
        share_rows = rounded(numer_owner / total_mass[..., None])
        owner_mass = rounded(total_mass)
        new_peak = jnp.maximum(row_peak, top_value)
        rescale = jnp.exp(row_peak - new_peak)
        factor = owner_mass * jnp.exp(top_value - new_peak)
        new_denominator = denominator * rescale + factor
        new_numerator = numerator * rescale[..., None] + factor[..., None] * share_rows
        return ((new_peak, new_denominator, new_numerator), None)
    owner_count = REQUESTS // R_DEV
    start = (own_top, own_total, own_numer)
    (row_peak, denominator, numerator), _ = lax.scan(owner_step, start, jnp.arange(owner_count, dtype=jnp.int32))
    attention = (numerator / denominator[..., None]).astype(jnp.bfloat16)
    attention = jnp.transpose(attention, (0, 2, 1, 3)).reshape(ROWS, D)
    projected = jnp.dot(attention, out_weight, preferred_element_type=jnp.float32)
    middle = (tokens.astype(jnp.float32) + projected).astype(jnp.bfloat16)
    normed_middle = normalize(middle, feedforward_gain)
    hidden = jax.nn.silu(jnp.dot(normed_middle, up_weight, preferred_element_type=jnp.float32)).astype(jnp.bfloat16)
    layer = middle.astype(jnp.float32) + jnp.dot(hidden, down_weight, preferred_element_type=jnp.float32)
    live_mask = (jnp.arange(SLOT)[None, :] < suffix_length[:, None]).reshape(ROWS)
    return jnp.where(live_mask[:, None], layer, 0.0).astype(jnp.bfloat16)
```

```python
import functools
import math

import jax
import jax.numpy as jnp
from jax import lax
from jax.experimental import pallas as pl
from jax.experimental.pallas import tpu as pltpu
from jax.sharding import Mesh
from jax.sharding import PartitionSpec as P

HDIM = 80
SLOT = 128
R_DEV = 2
PG = 192
LIVE = 192
CHIPS = 32
PREFIXES = 16
TP = 4
D = 1280
WIDTH = 320
HALF = 160
PAIR = 2 * LIVE
EXTRA = 8
EPSILON = 1e-06
NEGATIVE = -1e30
SCALE2 = math.log2(math.e) / math.sqrt(HDIM)
VMEM_LIMIT = 48 << 20


def normalize(values, gain):
    floats = values.astype(jnp.float32)
    mean_square = jnp.mean(floats * floats, axis=-1, keepdims=True)
    return (floats * lax.rsqrt(mean_square + EPSILON) * gain.astype(jnp.float32)).astype(
        jnp.bfloat16
    )


def dot(a, b, contract=((1,), (0,))):
    return lax.dot_general(a, b, (contract, ((), ())), preferred_element_type=jnp.float32)


def own_kernel(len_ref, q_ref, k_ref, v_ref, o_ref, lse_ref):
    first, second = len_ref[0], len_ref[1]
    key_row = lax.broadcasted_iota(jnp.int32, (LIVE, LIVE), 0)
    query_row = lax.broadcasted_iota(jnp.int32, (LIVE, LIVE), 1)

    def segment(row):
        return jnp.where(row < first, 0, jnp.where(row >= LIVE - second, 1, 2))

    valid = (key_row <= query_row) & (segment(key_row) == segment(query_row))
    for head in range(TP):
        rows = slice(head * HDIM, (head + 1) * HDIM)
        scores = dot(k_ref[rows, :], q_ref[rows, :], ((0,), (0,))) * SCALE2
        scores = jnp.where(valid, scores, NEGATIVE)
        top = jnp.max(scores, axis=0, keepdims=True)
        weights = jnp.exp2(scores - top)
        total = jnp.sum(weights, axis=0, keepdims=True)
        numer = dot(v_ref[rows, :], weights.astype(jnp.bfloat16))
        o_ref[rows, :] = numer / total
        lse_ref[pl.ds(head, 1), :] = top + jnp.log2(total)


def own_attention(lengths, queries, keys, values):
    return pl.pallas_call(
        own_kernel,
        out_shape=(
            jax.ShapeDtypeStruct((WIDTH, LIVE), jnp.float32),
            jax.ShapeDtypeStruct((TP, LIVE), jnp.float32),
        ),
        in_specs=[pl.BlockSpec(memory_space=pltpu.SMEM)]
        + [pl.BlockSpec(memory_space=pltpu.VMEM)] * 3,
        out_specs=(
            pl.BlockSpec(memory_space=pltpu.VMEM),
            pl.BlockSpec(memory_space=pltpu.VMEM),
        ),
        compiler_params=pltpu.CompilerParams(vmem_limit_bytes=VMEM_LIMIT),
        cost_estimate=pl.CostEstimate(
            flops=8 * LIVE * LIVE * HDIM * 2, transcendentals=4 * LIVE * LIVE, bytes_accessed=700000
        ),
        name="own_attention",
    )(lengths, queries, keys, values)


def split_rows(lse):
    high = lse.astype(jnp.bfloat16).astype(jnp.float32)
    rest = lse - high
    middle = rest.astype(jnp.bfloat16).astype(jnp.float32)
    low = rest - middle
    return high, middle, low


def cached_kernel(prefix_ref, len_ref, q_ref, k_ref, v_ref, o_ref):
    chip = pl.program_id(0)
    lane = lax.broadcasted_iota(jnp.int32, (HDIM, SLOT), 1)
    lane_row = lax.broadcasted_iota(jnp.int32, (1, SLOT), 1)
    low_half = lane < 64
    edge_first = jnp.maximum(len_ref[4 * chip], 64)
    edge_last = len_ref[4 * chip + 2] - 64
    lses = []
    for head in range(2):
        rows = slice(head * HDIM, (head + 1) * HDIM)
        tiles = [q_ref[0, rows, i * SLOT : (i + 1) * SLOT].astype(jnp.float32) for i in range(3)]
        windows = (
            tiles[0],
            jnp.where(low_half, tiles[1], tiles[0]),
            jnp.where(low_half, tiles[2], tiles[1]),
            tiles[2],
        )
        shares, tops = [], []
        for index in range(4):
            slot = 2 * prefix_ref[4 * chip + index] + head
            scores = dot(k_ref[slot], windows[index].astype(jnp.bfloat16)) * SCALE2
            top = jnp.max(scores, axis=0, keepdims=True)
            weights = jnp.exp2(scores - top)
            total = jnp.sum(weights, axis=0, keepdims=True)
            numer = dot(v_ref[slot], weights.astype(jnp.bfloat16))
            shares.append(numer / total)
            tops.append(top + jnp.log2(total))

        def merged(parts, at):
            return (
                jnp.where(at < edge_first, parts[0], parts[1]),
                jnp.where(at < 64, parts[1], parts[2]),
                jnp.where(at < edge_last, parts[2], parts[3]),
            )

        for i, part in enumerate(merged(shares, lane)):
            o_ref[0, rows, i * SLOT : (i + 1) * SLOT] = part.astype(jnp.bfloat16)
        lses.append(jnp.concatenate(merged(tops, lane_row), axis=1))
    pieces = [split_rows(lse) for lse in lses]
    sublane = lax.broadcasted_iota(jnp.int32, (EXTRA, PAIR), 0)
    extra = jnp.zeros((EXTRA, PAIR), jnp.float32)
    for kind in range(3):
        for head in range(2):
            extra = jnp.where(sublane == 2 * kind + head, pieces[head][kind], extra)
    o_ref[0, HALF : HALF + EXTRA, :] = extra.astype(jnp.bfloat16)


def cached_attention(prefixes, lengths, queries, keys, values):
    chips = queries.shape[0]
    return pl.pallas_call(
        cached_kernel,
        out_shape=jax.ShapeDtypeStruct((chips, HALF + EXTRA, PAIR), jnp.bfloat16),
        grid_spec=pltpu.PrefetchScalarGridSpec(
            num_scalar_prefetch=2,
            grid=(chips,),
            in_specs=[
                pl.BlockSpec((1, HALF, PAIR), lambda i, *_: (i, 0, 0)),
                pl.BlockSpec((2 * PREFIXES, 2 * PG, HDIM), lambda i, *_: (0, 0, 0)),
                pl.BlockSpec((2 * PREFIXES, HDIM, 2 * PG), lambda i, *_: (0, 0, 0)),
            ],
            out_specs=pl.BlockSpec((1, HALF + EXTRA, PAIR), lambda i, *_: (i, 0, 0)),
        ),
        compiler_params=pltpu.CompilerParams(
            dimension_semantics=("arbitrary",), vmem_limit_bytes=VMEM_LIMIT
        ),
        cost_estimate=pl.CostEstimate(
            flops=chips * 8 * 4 * SLOT * 2 * PG * HDIM,
            transcendentals=chips * 8 * SLOT * 2 * PG,
            bytes_accessed=chips * 260000 + 5000000,
        ),
        name="cached_attention",
    )(prefixes, lengths, queries, keys, values)


def combine_kernel(r_ref, o_ref):
    owners = r_ref.shape[0]

    def logs(owner):
        rows = r_ref[owner, HALF : HALF + EXTRA, :].astype(jnp.float32)
        return rows[0:2] + rows[2:4] + rows[4:6]

    lses = [logs(owner) for owner in range(owners)]
    peak = functools.reduce(jnp.maximum, lses)
    factors = [jnp.exp2(lse - peak) for lse in lses]
    total = functools.reduce(jnp.add, factors)
    for head in range(2):
        rows = slice(head * HDIM, (head + 1) * HDIM)
        acc = jnp.zeros((HDIM, PAIR), jnp.float32)
        for owner in range(owners):
            acc = acc + r_ref[owner, rows, :].astype(jnp.float32) * factors[owner][head : head + 1]
        o_ref[rows, :] = acc / total[head : head + 1]
    lse = peak + jnp.log2(total)
    o_ref[HALF : HALF + EXTRA, :] = jnp.concatenate(
        [lse, jnp.zeros((EXTRA - 2, PAIR), jnp.float32)], axis=0
    )


def combine(parts):
    return pl.pallas_call(
        combine_kernel,
        out_shape=jax.ShapeDtypeStruct((HALF + EXTRA, PAIR), jnp.float32),
        in_specs=[pl.BlockSpec(memory_space=pltpu.VMEM)],
        out_specs=pl.BlockSpec(memory_space=pltpu.VMEM),
        compiler_params=pltpu.CompilerParams(vmem_limit_bytes=VMEM_LIMIT),
        name="combine",
    )(parts)


def per_device(
    tokens,
    attention_gain,
    feedforward_gain,
    query_weight,
    key_weight,
    value_weight,
    out_weight,
    up_weight,
    down_weight,
    cache_keys,
    cache_values,
    request_prefix,
    suffix_length,
):
    core = lax.axis_index("core")
    chip = lax.axis_index("z") * 4 + lax.axis_index("x")
    is_first = core == 0
    swap = [(0, 1), (1, 0)]
    lengths = lax.dynamic_slice_in_dim(suffix_length, (chip * 2 + core) * R_DEV, R_DEV)
    first, second = lengths[0], lengths[1]

    row = lax.broadcasted_iota(jnp.int32, (LIVE, 2 * SLOT), 0)
    column = lax.broadcasted_iota(jnp.int32, (LIVE, 2 * SLOT), 1)
    picks = ((row < first) & (column == row)) | (
        (row >= LIVE - second) & (column == row - 64 + second)
    )
    picks = picks.astype(jnp.bfloat16)
    rows = dot(picks, tokens).astype(jnp.bfloat16)
    normed = normalize(rows, attention_gain)
    queries = dot(query_weight, normed, ((0,), (1,))).astype(jnp.bfloat16)

    other_half = jnp.where(is_first, queries[HALF:], queries[:HALF])
    mine = jnp.where(is_first, queries[:HALF], queries[HALF:])
    theirs = lax.ppermute(other_half, "core", swap)
    block = jnp.concatenate(
        [jnp.where(is_first, mine, theirs), jnp.where(is_first, theirs, mine)], axis=1
    )
    gathered = lax.all_gather(block, ("z", "x"), axis=0, tiled=False)

    def halves(cache):
        cache = cache[0]
        low, high = cache[..., :HALF], cache[..., HALF:]
        return jnp.where(is_first, low, high), lax.ppermute(
            jnp.where(is_first, high, low), "core", swap
        )

    keys_mine, keys_theirs = halves(cache_keys)
    values_mine, values_theirs = halves(cache_values)

    def by_head(part):
        return part.reshape(PREFIXES, PG, 2, HDIM)

    prefix_keys = jnp.concatenate([by_head(keys_mine), by_head(keys_theirs)], axis=1)
    prefix_keys = jnp.transpose(prefix_keys, (0, 2, 1, 3)).reshape(2 * PREFIXES, 2 * PG, HDIM)
    prefix_values = jnp.concatenate([by_head(values_mine), by_head(values_theirs)], axis=1)
    prefix_values = jnp.transpose(prefix_values, (0, 2, 3, 1)).reshape(2 * PREFIXES, HDIM, 2 * PG)

    keys_own = dot(key_weight, normed, ((0,), (1,))).astype(jnp.bfloat16)
    values_own = dot(value_weight, normed, ((0,), (1,))).astype(jnp.bfloat16)
    own_share, own_lse = own_attention(lengths, queries, keys_own, values_own)

    gathered, out_weight, up_weight, down_weight = lax.optimization_barrier(
        (gathered, out_weight, up_weight, down_weight)
    )
    out_full = lax.all_gather(out_weight, "tp", axis=0, tiled=True)
    up_full = lax.all_gather(up_weight, "tp", axis=0, tiled=False)
    down_full = lax.all_gather(down_weight, "tp", axis=0, tiled=True)

    parts = cached_attention(request_prefix, suffix_length, gathered, prefix_keys, prefix_values)
    parts = lax.all_to_all(parts, ("z", "x"), split_axis=0, concat_axis=0, tiled=True)
    joined = combine(parts)
    low, high = joined[:, :LIVE], joined[:, LIVE:]
    kept = jnp.where(is_first, low, high)
    came = lax.ppermute(jnp.where(is_first, high, low), "core", swap)
    even = jnp.where(is_first, kept, came)
    odd = jnp.where(is_first, came, kept)
    far_share = jnp.concatenate([even[:HALF], odd[:HALF]], axis=0)
    far_lse = jnp.concatenate([even[HALF : HALF + 2], odd[HALF : HALF + 2]], axis=0)
    peak = jnp.maximum(own_lse, far_lse)
    own_factor = jnp.exp2(own_lse - peak)
    far_factor = jnp.exp2(far_lse - peak)
    total = own_factor + far_factor
    attention = (
        own_share.reshape(TP, HDIM, LIVE) * (own_factor / total)[:, None]
        + far_share.reshape(TP, HDIM, LIVE) * (far_factor / total)[:, None]
    ).astype(jnp.bfloat16)
    piece = LIVE // TP
    attention = jnp.transpose(attention.reshape(WIDTH, TP, piece), (1, 2, 0))
    attention = lax.all_to_all(attention, "tp", split_axis=0, concat_axis=0, tiled=True)
    attention = jnp.transpose(attention, (1, 0, 2)).reshape(piece, D)

    tensor_index = lax.axis_index("tp")
    rows_mine = lax.dynamic_slice_in_dim(rows, tensor_index * piece, piece, 0)
    middle = (rows_mine.astype(jnp.float32) + dot(attention, out_full)).astype(jnp.bfloat16)
    normed_middle = normalize(middle, feedforward_gain)
    hidden = jnp.einsum(
        "rd,tdf->rtf", normed_middle, up_full, preferred_element_type=jnp.float32
    )
    hidden = jax.nn.silu(hidden).astype(jnp.bfloat16).reshape(piece, D)
    layer = (middle.astype(jnp.float32) + dot(hidden, down_full)).astype(jnp.bfloat16)
    layer = jnp.transpose(layer.reshape(piece, TP, WIDTH), (1, 0, 2))
    layer = lax.all_to_all(layer, "tp", split_axis=0, concat_axis=0, tiled=True)
    layer = layer.reshape(LIVE, WIDTH)
    return dot(picks, layer, ((0,), (0,))).astype(jnp.bfloat16)


def solution(mesh):
    wide = Mesh(mesh.devices.reshape(8, 4, 2, TP), ("z", "x", "core", "tp"))
    req = ("z", "x", "core")
    in_specs = (
        P(req, None),
        P(),
        P(),
        P(None, "tp"),
        P(None, "tp"),
        P(None, "tp"),
        P("tp", None),
        P(None, "tp"),
        P("tp", None),
        P(req, None, None, "tp"),
        P(req, None, None, "tp"),
        P(),
        P(),
    )
    out_specs = P(req, "tp")
    return jax.shard_map(
        per_device, mesh=wide, in_specs=in_specs, out_specs=out_specs, check_vma=False
    )
```

```python
import functools
import math

import jax
import jax.numpy as jnp
from jax import lax
from jax.experimental import pallas as pl
from jax.experimental.pallas import tpu as pltpu
from jax.sharding import Mesh
from jax.sharding import PartitionSpec as P

HDIM = 80
SLOT = 128
R_DEV = 2
PG = 192
LIVE = 192
CHIPS = 32
PREFIXES = 16
TP = 4
D = 1280
WIDTH = 320
HALF = 160
PAIR = 2 * LIVE
EXTRA = 8
EPSILON = 1e-06
NEGATIVE = -1e30
SCALE2 = math.log2(math.e) / math.sqrt(HDIM)
VMEM_LIMIT = 48 << 20


def normalize(values, gain):
    floats = values.astype(jnp.float32)
    mean_square = jnp.mean(floats * floats, axis=-1, keepdims=True)
    return (floats * lax.rsqrt(mean_square + EPSILON) * gain.astype(jnp.float32)).astype(
        jnp.bfloat16
    )


def dot(a, b, contract=((1,), (0,))):
    return lax.dot_general(a, b, (contract, ((), ())), preferred_element_type=jnp.float32)


def own_kernel(len_ref, q_ref, k_ref, v_ref, o_ref, lse_ref):
    first, second = len_ref[0], len_ref[1]
    key_row = lax.broadcasted_iota(jnp.int32, (LIVE, LIVE), 0)
    query_row = lax.broadcasted_iota(jnp.int32, (LIVE, LIVE), 1)

    def segment(row):
        return jnp.where(row < first, 0, jnp.where(row >= LIVE - second, 1, 2))

    valid = (key_row <= query_row) & (segment(key_row) == segment(query_row))
    for head in range(TP):
        rows = slice(head * HDIM, (head + 1) * HDIM)
        scores = dot(k_ref[rows, :], q_ref[rows, :], ((0,), (0,))) * SCALE2
        scores = jnp.where(valid, scores, NEGATIVE)
        top = jnp.max(scores, axis=0, keepdims=True)
        weights = jnp.exp2(scores - top)
        total = jnp.sum(weights, axis=0, keepdims=True)
        numer = dot(v_ref[rows, :], weights.astype(jnp.bfloat16))
        o_ref[rows, :] = numer / total
        lse_ref[pl.ds(head, 1), :] = top + jnp.log2(total)


def own_attention(lengths, queries, keys, values):
    return pl.pallas_call(
        own_kernel,
        out_shape=(
            jax.ShapeDtypeStruct((WIDTH, LIVE), jnp.float32),
            jax.ShapeDtypeStruct((TP, LIVE), jnp.float32),
        ),
        in_specs=[pl.BlockSpec(memory_space=pltpu.SMEM)]
        + [pl.BlockSpec(memory_space=pltpu.VMEM)] * 3,
        out_specs=(
            pl.BlockSpec(memory_space=pltpu.VMEM),
            pl.BlockSpec(memory_space=pltpu.VMEM),
        ),
        compiler_params=pltpu.CompilerParams(vmem_limit_bytes=VMEM_LIMIT),
        cost_estimate=pl.CostEstimate(
            flops=8 * LIVE * LIVE * HDIM * 2, transcendentals=4 * LIVE * LIVE, bytes_accessed=700000
        ),
        name="own_attention",
    )(lengths, queries, keys, values)


def split_rows(lse):
    high = lse.astype(jnp.bfloat16).astype(jnp.float32)
    rest = lse - high
    middle = rest.astype(jnp.bfloat16).astype(jnp.float32)
    low = rest - middle
    return high, middle, low


def any_vmem(count):
    return [pl.BlockSpec(memory_space=pltpu.VMEM)] * count


def prepare_kernel(core_ref, k_ref, v_ref, km_ref, ks_ref, vm_ref, vs_ref):
    first = core_ref[0] == 0
    keys = k_ref[0].astype(jnp.float32)
    low, high = keys[:, :HALF], keys[:, HALF:]
    km_ref[0] = jnp.where(first, low, high).astype(jnp.bfloat16)
    ks_ref[0] = jnp.where(first, high, low).astype(jnp.bfloat16)
    values = v_ref[0].astype(jnp.float32).T
    low, high = values[:HALF], values[HALF:]
    vm_ref[0] = jnp.where(first, low, high).astype(jnp.bfloat16)
    vs_ref[0] = jnp.where(first, high, low).astype(jnp.bfloat16)


def prepare(core, keys, values):
    key_out = jax.ShapeDtypeStruct((PREFIXES, PG, HALF), jnp.bfloat16)
    value_out = jax.ShapeDtypeStruct((PREFIXES, HALF, PG), jnp.bfloat16)
    key_spec = pl.BlockSpec((1, PG, HALF), lambda i: (i, 0, 0))
    value_spec = pl.BlockSpec((1, HALF, PG), lambda i: (i, 0, 0))
    in_spec = pl.BlockSpec((1, PG, WIDTH), lambda i: (i, 0, 0))
    return pl.pallas_call(
        prepare_kernel,
        out_shape=(key_out, key_out, value_out, value_out),
        grid=(PREFIXES,),
        in_specs=[pl.BlockSpec(memory_space=pltpu.SMEM), in_spec, in_spec],
        out_specs=(key_spec, key_spec, value_spec, value_spec),
        compiler_params=pltpu.CompilerParams(vmem_limit_bytes=VMEM_LIMIT),
        cost_estimate=pl.CostEstimate(flops=0, transcendentals=0, bytes_accessed=10000000),
        name="prepare",
    )(core, keys, values)


def store_packed(shares, logs, o_ref, at):
    sublane = lax.broadcasted_iota(jnp.int32, (EXTRA, SLOT), 0)
    for i in range(3):
        lanes = slice(i * SLOT, (i + 1) * SLOT)
        o_ref[at + (slice(0, HALF), lanes)] = shares[i].astype(jnp.bfloat16)
        extra = jnp.zeros((EXTRA, SLOT), jnp.float32)
        for head in range(2):
            for kind, piece in enumerate(split_rows(logs[i][head])):
                extra = jnp.where(sublane == 2 * kind + head, piece, extra)
        o_ref[at + (slice(HALF, HALF + EXTRA), lanes)] = extra.astype(jnp.bfloat16)


def cached_kernel(
    shifts, place_ref, prefix_ref, len_ref, *refs
):
    planes = len(shifts)
    q_refs = refs[:planes]
    ka_ref, kb_ref, va_ref, vb_ref, o_ref, s_ref, p_ref = refs[planes:]
    slot = pl.program_id(0)
    lane = lax.broadcasted_iota(jnp.int32, (HALF, SLOT), 1)
    upper = lax.broadcasted_iota(jnp.int32, (HALF, SLOT), 0) >= HDIM
    lane_row = lax.broadcasted_iota(jnp.int32, (1, SLOT), 1)
    low_half = lane < 64
    zero = jnp.zeros((HALF, SLOT), jnp.float32)
    chips = [
        ((place_ref[0] + shift + 8) % 8) * 4 + (place_ref[1] + 4 - slot) % 4 for shift in shifts
    ]
    units = [(plane, index) for plane in range(planes) for index in range(4)]
    tops, totals, shares, logs = {}, {}, {}, {}

    def prefix_of(unit):
        return prefix_ref[4 * chips[unit[0]] + unit[1]]

    def score(at):
        unit = units[at]
        plane, index = unit
        tiles = [
            q_refs[plane][0, :, i * SLOT : (i + 1) * SLOT].astype(jnp.float32)
            for i in ((0,), (0, 1), (1, 2), (2,))[index]
        ]
        window = tiles[0] if len(tiles) == 1 else jnp.where(low_half, tiles[1], tiles[0])
        pair = jnp.concatenate(
            [jnp.where(upper, zero, window), jnp.where(upper, window, zero)], axis=1
        ).astype(jnp.bfloat16)
        prefix = prefix_of(unit)
        first = dot(ka_ref[prefix], pair)
        s_ref[at, :PG] = first
        second = dot(kb_ref[prefix], pair)
        s_ref[at, PG:] = second
        tops[at] = jnp.maximum(
            jnp.max(first, axis=0, keepdims=True), jnp.max(second, axis=0, keepdims=True)
        )

    def weigh(at):
        top = tops[at] * SCALE2
        total = jnp.zeros((8, 2 * SLOT), jnp.float32)
        for part in range(4):
            rows = slice(part * 96, (part + 1) * 96)
            weights = jnp.exp2(s_ref[at, rows] * SCALE2 - top)
            total = total + jnp.sum(weights.reshape(12, 8, 2 * SLOT), axis=0)
            p_ref[at, rows] = weights.astype(jnp.bfloat16)
        totals[at] = jnp.sum(total, axis=0, keepdims=True)

    def gather(at):
        prefix = prefix_of(units[at])
        numer = dot(va_ref[prefix], p_ref[at, :PG]) + dot(vb_ref[prefix], p_ref[at, PG:])
        inverse = 1.0 / totals[at]
        shares[units[at]] = jnp.where(
            upper, numer[:, SLOT:] * inverse[:, SLOT:], numer[:, :SLOT] * inverse[:, :SLOT]
        )
        log = tops[at] * SCALE2 + jnp.log2(totals[at])
        logs[units[at]] = (log[:, :SLOT], log[:, SLOT:])

    for step in range(len(units) + 2):
        if step < len(units):
            score(step)
        if 0 <= step - 1 < len(units):
            weigh(step - 1)
        if 0 <= step - 2:
            gather(step - 2)

    for plane in range(planes):
        edge_first = jnp.maximum(len_ref[4 * chips[plane]], 64)
        edge_last = len_ref[4 * chips[plane] + 2] - 64

        def merged(parts, at):
            return (
                jnp.where(at < edge_first, parts[0], parts[1]),
                jnp.where(at < 64, parts[1], parts[2]),
                jnp.where(at < edge_last, parts[2], parts[3]),
            )

        by_head = [
            merged([logs[plane, index][head] for index in range(4)], lane_row)
            for head in range(2)
        ]
        store_packed(
            merged([shares[plane, index] for index in range(4)], lane),
            [(by_head[0][i], by_head[1][i]) for i in range(3)],
            o_ref,
            (0, plane),
        )


def cached_attention(shifts, place, prefixes, lengths, queries, cache):
    planes = len(shifts)
    q_spec = pl.BlockSpec((1, HALF, PAIR), lambda i, *_: (i, 0, 0))
    whole = [
        pl.BlockSpec(array.shape, lambda i, *_: (0, 0, 0), pipeline_mode=pl.Buffered(1))
        for array in cache
    ]
    units = 4 * planes
    return pl.pallas_call(
        functools.partial(cached_kernel, shifts),
        out_shape=jax.ShapeDtypeStruct((4, planes, HALF + EXTRA, PAIR), jnp.bfloat16),
        grid_spec=pltpu.PrefetchScalarGridSpec(
            num_scalar_prefetch=3,
            grid=(4,),
            in_specs=[q_spec] * planes + whole,
            out_specs=pl.BlockSpec((1, planes, HALF + EXTRA, PAIR), lambda i, *_: (i, 0, 0, 0)),
            scratch_shapes=[
                pltpu.VMEM((units, 2 * PG, 2 * SLOT), jnp.float32),
                pltpu.VMEM((units, 2 * PG, 2 * SLOT), jnp.bfloat16),
            ],
        ),
        compiler_params=pltpu.CompilerParams(
            dimension_semantics=("arbitrary",), vmem_limit_bytes=VMEM_LIMIT
        ),
        cost_estimate=pl.CostEstimate(
            flops=planes * 4000000000,
            transcendentals=planes * 16 * 2 * PG * 2 * SLOT,
            bytes_accessed=planes * 2000000,
        ),
        name="cached_attention",
    )(place, prefixes, lengths, *queries, *cache)


def join(parts):
    logs = []
    for read in parts:
        rows = read(slice(HALF, HALF + EXTRA)).astype(jnp.float32)
        logs.append(rows[0:2] + rows[2:4] + rows[4:6])
    peak = functools.reduce(jnp.maximum, logs)
    factors = [jnp.exp2(log - peak) for log in logs]
    total = functools.reduce(jnp.add, factors)
    shares = []
    for head in range(2):
        rows = slice(head * HDIM, (head + 1) * HDIM)
        acc = sum(
            read(rows).astype(jnp.float32) * factor[head : head + 1]
            for read, factor in zip(parts, factors)
        )
        shares.append(acc * (1.0 / total[head : head + 1]))
    return shares, peak + jnp.log2(total)


def join_kernel(planes, own_ref, *refs):
    o_refs = refs[3:]
    for plane in range(planes):
        reads = [lambda rows, ref=ref: ref[plane, rows, :] for ref in (own_ref,) + refs[:3]]
        shares, log = join(reads)
        for head in range(2):
            o_refs[plane][head * HDIM : (head + 1) * HDIM, :] = shares[head].astype(jnp.bfloat16)
        pieces = split_rows(log)
        sublane = lax.broadcasted_iota(jnp.int32, (EXTRA, PAIR), 0)
        extra = jnp.zeros((EXTRA, PAIR), jnp.float32)
        for kind in range(3):
            for head in range(2):
                extra = jnp.where(
                    sublane == 2 * kind + head, pieces[kind][head : head + 1], extra
                )
        o_refs[plane][HALF:, :] = extra.astype(jnp.bfloat16)


def join_planes(parts):
    planes = parts[0].shape[0]
    return pl.pallas_call(
        functools.partial(join_kernel, planes),
        out_shape=[jax.ShapeDtypeStruct((HALF + EXTRA, PAIR), jnp.bfloat16)] * planes,
        in_specs=any_vmem(4),
        out_specs=any_vmem(planes),
        compiler_params=pltpu.CompilerParams(vmem_limit_bytes=VMEM_LIMIT),
        cost_estimate=pl.CostEstimate(
            flops=planes * 500000, transcendentals=0, bytes_accessed=planes * 700000
        ),
        name="join_planes",
    )(*parts)


def final_kernel(core_ref, *refs):
    kept_ref, sent_ref = refs[-2:]
    first = core_ref[0] == 0
    shares, log = join([lambda rows, ref=ref: ref[rows, :] for ref in refs[:-2]])
    tail = jnp.concatenate([log, jnp.zeros((EXTRA - 2, PAIR), jnp.float32)], axis=0)
    joined = jnp.concatenate(shares + [tail], axis=0)
    low, high = joined[:, :LIVE], joined[:, LIVE:]
    kept_ref[...] = jnp.where(first, low, high)
    sent_ref[...] = jnp.where(first, high, low)


def final_join(core, parts):
    return pl.pallas_call(
        final_kernel,
        out_shape=[jax.ShapeDtypeStruct((HALF + EXTRA, LIVE), jnp.float32)] * 2,
        in_specs=[pl.BlockSpec(memory_space=pltpu.SMEM)] + any_vmem(len(parts)),
        out_specs=any_vmem(2),
        compiler_params=pltpu.CompilerParams(vmem_limit_bytes=VMEM_LIMIT),
        name="final_join",
    )(core, *parts)


def merge_kernel(core_ref, kept_ref, came_ref, share_ref, log_ref, o_ref):
    core = core_ref[0]
    piece = LIVE // TP
    for part, far_ref in enumerate((kept_ref, came_ref)):
        base = core if part == 0 else 1 - core
        own = share_ref[pl.ds(pl.multiple_of(base * HALF, 16), HALF), :]
        blocks = []
        for head in range(2):
            rows = slice(head * HDIM, (head + 1) * HDIM)
            own_log = log_ref[pl.ds(base * 2 + head, 1), :]
            far_log = far_ref[HALF + head : HALF + head + 1, :]
            peak = jnp.maximum(own_log, far_log)
            own_factor = jnp.exp2(own_log - peak)
            far_factor = jnp.exp2(far_log - peak)
            inverse = 1.0 / (own_factor + far_factor)
            blocks.append(
                own[rows] * (own_factor * inverse) + far_ref[rows, :] * (far_factor * inverse)
            )
        turned = jnp.concatenate(blocks, axis=0).T.astype(jnp.bfloat16)
        for i in range(TP):
            o_ref[i, part] = turned[i * piece : (i + 1) * piece]


def merge(core, kept, came, share, log):
    return pl.pallas_call(
        merge_kernel,
        out_shape=jax.ShapeDtypeStruct((TP, 2, LIVE // TP, HALF), jnp.bfloat16),
        in_specs=[pl.BlockSpec(memory_space=pltpu.SMEM)] + any_vmem(4),
        out_specs=any_vmem(1)[0],
        compiler_params=pltpu.CompilerParams(vmem_limit_bytes=VMEM_LIMIT),
        name="merge_own",
    )(core, kept, came, share, log)


def tail_kernel(spans, rows_ref, gain_ref, *refs):
    o_ref = refs[-1]
    attention = refs[:TP]
    weights = refs[TP:-1]
    middle = rows_ref[...].astype(jnp.float32)
    for (source, part, low, high), ref in zip(spans, weights):
        middle = middle + dot(attention[source][part][:, low:high], ref[0])
    middle = middle.astype(jnp.bfloat16)
    floats = middle.astype(jnp.float32)
    mean_square = jnp.mean(floats * floats, axis=-1, keepdims=True)
    normed = (floats * lax.rsqrt(mean_square + EPSILON) * gain_ref[...].astype(jnp.float32)).astype(
        jnp.bfloat16
    )
    layer = floats
    for ref in weights:
        value = dot(normed, ref[1], ((1,), (1,)))
        hidden = (value / (1.0 + jnp.exp(-value))).astype(jnp.bfloat16)
        layer = layer + dot(hidden, ref[2])
    layer = layer.astype(jnp.bfloat16)
    for i in range(TP):
        o_ref[i] = layer[:, i * WIDTH : (i + 1) * WIDTH]


def tail(spans, rows, gain, attention, weights):
    piece = LIVE // TP
    return pl.pallas_call(
        functools.partial(tail_kernel, spans),
        out_shape=jax.ShapeDtypeStruct((TP, piece, WIDTH), jnp.bfloat16),
        in_specs=any_vmem(2 + TP + len(weights)),
        out_specs=any_vmem(1)[0],
        compiler_params=pltpu.CompilerParams(vmem_limit_bytes=VMEM_LIMIT),
        name="tail",
    )(rows, gain, *attention, *weights)


def shift(array, axis, by, size):
    return lax.ppermute(array, axis, [(i, (i + by) % size) for i in range(size)])


def per_device(
    tokens,
    attention_gain,
    feedforward_gain,
    query_weight,
    key_weight,
    value_weight,
    out_weight,
    up_weight,
    down_weight,
    cache_keys,
    cache_values,
    request_prefix,
    suffix_length,
):
    core, tensor = lax.axis_index("core"), lax.axis_index("tp")
    place = jnp.stack([lax.axis_index("z"), lax.axis_index("x")])
    core_of = core.reshape(1)
    chip = lax.axis_index("z") * 4 + lax.axis_index("x")
    is_first = core == 0
    lengths = lax.dynamic_slice_in_dim(suffix_length, (chip * 2 + core) * R_DEV, R_DEV)
    first, second = lengths[0], lengths[1]

    def picks_at(row):
        column = lax.broadcasted_iota(jnp.int32, (LIVE, 2 * SLOT), 1)
        picked = ((row < first) & (column == row)) | (
            (row >= LIVE - second) & (column == row - 64 + second)
        )
        return picked.astype(jnp.bfloat16)

    row = lax.broadcasted_iota(jnp.int32, (LIVE, 2 * SLOT), 0)
    rows = dot(picks_at(row), tokens).astype(jnp.bfloat16)
    normed = normalize(rows, attention_gain)
    queries = dot(query_weight, normed, ((0,), (1,))).astype(jnp.bfloat16)

    def swap(array):
        return lax.ppermute(array, "core", [(0, 1), (1, 0)])

    other_half = jnp.where(is_first, queries[HALF:], queries[:HALF])
    mine = jnp.where(is_first, queries[:HALF], queries[HALF:])
    theirs = swap(other_half)
    block = jnp.concatenate(
        [jnp.where(is_first, mine, theirs), jnp.where(is_first, theirs, mine)], axis=1
    )

    keys_mine, keys_sent, values_mine, values_sent = prepare(
        core_of, cache_keys[0], cache_values[0]
    )
    cache = (keys_mine, swap(keys_sent), values_mine, swap(values_sent))

    bundle = jnp.stack(
        [block, shift(block, "x", 1, 4), shift(block, "x", 2, 4), shift(block, "x", -1, 4)]
    )

    def attend(shifts, queries):
        results = cached_attention(shifts, place, request_prefix, suffix_length, queries, cache)
        return join_planes(
            [results[0]] + [shift(results[i], "x", -i, 4) for i in range(1, 4)]
        )

    parts = list(attend((0,), (bundle,)))
    up, down = bundle, bundle
    for step in range(1, 4):
        up, down = shift(up, "z", 1, 8), shift(down, "z", -1, 8)
        behind, ahead = attend((-step, step), (up, down))
        parts = parts + [shift(behind, "z", -step, 8), shift(ahead, "z", step, 8)]
    far = jnp.concatenate([shift(up[:2], "z", 1, 8), shift(down[2:], "z", -1, 8)], axis=0)
    (opposite,) = attend((4,), (far,))
    parts = parts + [shift(opposite, "z", 4, 8)]

    keys_own = dot(key_weight, normed, ((0,), (1,))).astype(jnp.bfloat16)
    values_own = dot(value_weight, normed, ((0,), (1,))).astype(jnp.bfloat16)
    own_share, own_log = own_attention(lengths, queries, keys_own, values_own)

    stacked = jnp.stack([out_weight, up_weight.T, down_weight])
    low, high = stacked[:, :HALF], stacked[:, HALF:]
    half_mine, half_theirs = jnp.where(is_first, low, high), jnp.where(is_first, high, low)
    before, after = shift(half_mine, "tp", 1, TP), shift(half_mine, "tp", -1, TP)
    across_low = shift(before[:, :HDIM], "tp", 1, TP)
    across_high = shift(after[:, HDIM:], "tp", -1, TP)
    weights, spans = [half_mine, half_theirs], [(0, 0, 0, HALF), (0, 1, 0, HALF)]
    for source, array, low, high in (
        (1, before, 0, HALF),
        (3, after, 0, HALF),
        (2, across_low, 0, HDIM),
        (2, across_high, HDIM, HALF),
    ):
        weights += [array, swap(array)]
        spans += [(source, 0, low, high), (source, 1, low, high)]

    kept, sent = final_join(core_of, parts)
    pieces = merge(core_of, kept, swap(sent), own_share, own_log)

    def exchange(pieces):
        return [
            shift(
                lax.dynamic_index_in_dim(pieces, (tensor + by) % TP, 0, keepdims=False),
                "tp",
                by,
                TP,
            )
            if by
            else lax.dynamic_index_in_dim(pieces, tensor, 0, keepdims=False)
            for by in range(TP)
        ]

    piece = LIVE // TP
    rows_mine = lax.dynamic_slice_in_dim(rows, tensor * piece, piece, 0)
    layer = tail(
        tuple(spans), rows_mine, feedforward_gain.reshape(1, D), exchange(pieces), weights
    )
    layer = jnp.concatenate(exchange(layer), axis=0)
    source = (tensor + TP - row // piece) % TP
    placed = picks_at(source * piece + row % piece)
    return dot(placed, layer, ((0,), (0,))).astype(jnp.bfloat16)


def solution(mesh):
    wide = Mesh(mesh.devices.reshape(8, 4, 2, TP), ("z", "x", "core", "tp"))
    req = ("z", "x", "core")
    in_specs = (
        P(req, None),
        P(),
        P(),
        P(None, "tp"),
        P(None, "tp"),
        P(None, "tp"),
        P("tp", None),
        P(None, "tp"),
        P("tp", None),
        P(req, None, None, "tp"),
        P(req, None, None, "tp"),
        P(),
        P(),
    )
    out_specs = P(req, "tp")
    return jax.shard_map(
        per_device, mesh=wide, in_specs=in_specs, out_specs=out_specs, check_vma=False
    )
```
